128 devices in a mesh: grp: 8 (over y, core), mig: 4 (over x), pen: 4 (over z).
Axes of the slice: x: 4, y: 4, z: 4, core: 2. Of those that a mesh axis runs over, the one named last changes fastest.
Arguments:
- fields: float32 [4096, 9, 4096], P(('grp', 'mig', 'pen')), may hold values from -6 to 6
- ghosts: float32 [4096, 9, 1536], P(('grp', 'mig', 'pen')), may hold values from -6 to 6
- velocity: float32 [3, 4096], P(None, ('grp', 'mig', 'pen')), may hold values from -1 to 1
- rate_matrix: float32 [9, 9], replicated, may hold values from -2 to 2
- recent_tend: bfloat16 [4096, 9, 4096], P(('grp', 'mig', 'pen')), may hold values from -6 to 6
- older_tend: bfloat16 [4096, 9, 4096], P(('grp', 'mig', 'pen')), may hold values from -6 to 6
- destination: int32 [4096], P(('grp', 'mig', 'pen')), may hold values from 0 to 15, as said below
- target_slot: int32 [4096], P(('grp', 'mig', 'pen')), may hold values from 0 to 32, as said below
- live_counts: int32 [128], P(('grp', 'mig', 'pen')), may hold values from 0 to 32, as said below
- tile_ids: int32 [4096], P(('grp', 'mig', 'pen')), may hold values from 0 to 4095, each once
- sensor: float32 [128, 131072], P('pen', ('grp', 'mig')), may hold values from 0 to 4
- flame_flags: int32 [8, 512], P('pen', ('grp', 'mig')), may hold values 0 or 1
Outputs:
- new_fields: float32 [4096, 9, 4096], P(('grp', 'mig', 'pen'))
- new_tend: bfloat16 [4096, 9, 4096], P(('grp', 'mig', 'pen'))
- filtered: float32 [128, 131072], P('pen', ('grp', 'mig'))
The draws below stay inside these ranges and needn't reach their ends.
Inputs may be any that keep to these rules, and one draw needn't show every extreme that they name: `destination`: index (mig-major) within the old slot's group of devices sharing its grp index; a device names every other device of its group for at most one of its slots; slots whose tile stays, and slots without a tile, name the device itself. `target_slot`: 32 marks an old slot without a tile; at each device the kept and arriving tiles take the slots 0 to its live count - 1, each exactly once. `live_counts`: equals the number of tiles that a device keeps or receives.
All inputs are finite; a program needn't handle non-finite values. No bound on the sum of `flame_flags` on one device may be relied on, other than what follows from the above.
Results may differ from the reference program's by a relative error of at most 0.001.
Values may be sent and summed in bfloat16 or wider, within the bound.
A program may use at most 320 MiB of HBM per device.

```python
import jax
import jax.numpy as jnp
from jax import lax

S = 9
TE = 16
TZ = 2
TCOL = 16
SLOTS = 32
NTILES = 4096
BZ = 32
NZ = 128
NCOL = 131072
NTZ = 8
NTC = 512
N_GRP = 8
N_MIG = 4
N_PEN = 4


def migration_plan(key):
    peer_count = N_MIG * N_PEN
    groups = N_GRP
    subkeys = jax.random.split(jax.random.fold_in(key, 911), 6)
    members = jnp.arange(peer_count, dtype=jnp.int32)
    rank_list = jnp.arange(SLOTS, dtype=jnp.int32)
    thresholds = jax.random.randint(subkeys[0], (groups, peer_count), 0, 5)
    chosen = jax.random.randint(subkeys[1], (groups,), 0, peer_count)
    is_full = members[None, :] == chosen[:, None]
    is_empty = members[None, :] == (chosen[:, None] + 1) % peer_count
    thresholds = jnp.where(is_full, 4, thresholds)
    throws = jax.random.randint(subkeys[2], (groups, peer_count, peer_count), 0, 4)
    self_link = members[:, None] == members[None, :]
    linkage = ((throws < thresholds[:, None, :]) & jnp.logical_not(self_link)[None]).astype(jnp.int32)
    out_degree = jnp.sum(linkage, axis=2)
    in_degree = jnp.sum(linkage, axis=1)
    headroom = SLOTS - jnp.maximum(out_degree, in_degree)
    staying = jax.random.randint(subkeys[3], (groups, peer_count), 0, headroom + 1)
    staying = jnp.where(is_full, headroom, staying)
    staying = jnp.where(is_empty, 0, staying)
    counts = staying + in_degree
    old_scores = jax.random.randint(subkeys[4], (groups, peer_count, SLOTS), 0, 1 << 20) * SLOTS + rank_list
    old_order = jnp.argsort(old_scores, axis=2)
    rank_of_slot = jnp.argsort(old_order, axis=2)
    receivers = jnp.argsort((1 - linkage) * peer_count + members[None, None, :], axis=2)
    arriving = jnp.cumsum(linkage, axis=1) - linkage
    new_scores = jax.random.randint(subkeys[5], (groups, peer_count, SLOTS), 0, 1 << 20) * SLOTS + rank_list
    new_order = jnp.argsort(new_scores, axis=2)
    sort_key = jnp.where(new_order < counts[:, :, None], rank_list, SLOTS + rank_list)
    layout = jnp.take_along_axis(new_order, jnp.argsort(sort_key, axis=2), axis=2)
    is_send = rank_list[None, None, :] < out_degree[:, :, None]
    is_keep = jnp.logical_not(is_send) & (rank_list[None, None, :] < (out_degree + staying)[:, :, None])
    clipped_rank = jnp.broadcast_to(jnp.minimum(rank_list, peer_count - 1), (groups, peer_count, SLOTS))
    target_peer = jnp.take_along_axis(receivers, clipped_rank, axis=2)
    staying_wide = jnp.broadcast_to(staying[:, None, :], (groups, peer_count, peer_count))
    position = jnp.take_along_axis(arriving, target_peer, axis=2) + jnp.take_along_axis(staying_wide, target_peer, axis=2)
    flat_layout = layout.reshape(groups, peer_count * SLOTS)
    pick_index = (target_peer * SLOTS + jnp.minimum(position, SLOTS - 1)).reshape(groups, peer_count * SLOTS)
    sent_slot = jnp.take_along_axis(flat_layout, pick_index, axis=1).reshape(groups, peer_count, SLOTS)
    kept_rank = jnp.clip(rank_list[None, None, :] - out_degree[:, :, None], 0, SLOTS - 1)
    kept_slot = jnp.take_along_axis(layout, kept_rank, axis=2)
    slot_by_rank = jnp.where(is_send, sent_slot, jnp.where(is_keep, kept_slot, SLOTS))
    peer_by_rank = jnp.where(is_send, target_peer, members[None, :, None])
    destination = jnp.take_along_axis(peer_by_rank, rank_of_slot, axis=2)
    target = jnp.take_along_axis(slot_by_rank, rank_of_slot, axis=2)
    return (destination.reshape(-1).astype(jnp.int32), target.reshape(-1).astype(jnp.int32), counts.reshape(-1).astype(jnp.int32))


def draw_destination(key, part):
    return migration_plan(key)[0]


def draw_target_slot(key, part):
    return migration_plan(key)[1]


def draw_live_counts(key, part):
    return migration_plan(key)[2]


def plant(array, stream_key, least, top_value):
    longest = array.shape.index(max(array.shape))
    spots = []
    for shift in (0, 1):
        where = [jax.random.randint(jax.random.fold_in(stream_key, axis), (), 0, length) for axis, length in enumerate(array.shape)]
        where[longest] = (where[longest] + shift) % array.shape[longest]
        spots.append(tuple(where))
    return array.at[spots[0]].set(least).at[spots[1]].set(top_value)


def block_scale(own_key, dims, cuts, least, top_value):
    loudness, own = 1.0, jax.random.fold_in(own_key, 6)
    for axis_at, parts in cuts:
        steps = jnp.exp(jax.random.uniform(jax.random.fold_in(own, axis_at), (parts,), jnp.float32, least / len(cuts), top_value / len(cuts)))
        loudness = loudness * jnp.repeat(steps, dims[axis_at] // parts).reshape([-1 if axis == axis_at else 1 for axis in range(len(dims))])
    return loudness


def bell_draw(rng, dims, scale, most, cuts=(), kind=jnp.bfloat16):
    array = jax.random.normal(rng, dims, jnp.float32) * scale
    if len(cuts) > 0:
        array = block_scale(rng, dims, cuts, -0.22, 0.18) * array
    return jnp.clip(array, min=-most, max=most).astype(kind)


def setup_inputs(seed: int = 0) -> dict:
    arg_keys = jax.random.split(jax.random.key(seed), 13)
    return {
        "fields": bell_draw(arg_keys[0], (NTILES, S, TE**3), 1.0, 6.0, ((0, 128),), jnp.float32),
        "ghosts": bell_draw(arg_keys[1], (NTILES, S, 6 * TE * TE), 1.0, 6.0, ((0, 128),), jnp.float32),
        "velocity": jnp.clip(jax.random.uniform(arg_keys[2], (3, NTILES), jnp.float32, -1.0, 1.0) * block_scale(arg_keys[2], (3, NTILES), ((1, 128),), -0.4, 0.0), -1.0, 1.0),
        "rate_matrix": bell_draw(arg_keys[3], (S, S), S ** -0.5, 2.0, (), jnp.float32),
        "recent_tend": bell_draw(arg_keys[4], (NTILES, S, TE**3), 1.0, 6.0, ((0, 128),)),
        "older_tend": bell_draw(arg_keys[5], (NTILES, S, TE**3), 1.0, 6.0, ((0, 128),)),
        "destination": draw_destination(jax.random.fold_in(arg_keys[12], 71), 0),
        "target_slot": draw_target_slot(jax.random.fold_in(arg_keys[12], 71), 0),
        "live_counts": draw_live_counts(jax.random.fold_in(arg_keys[12], 71), 0),
        "tile_ids": jax.random.permutation(arg_keys[9], NTILES).astype(jnp.int32),
        "sensor": jnp.clip(4.0 * jax.random.uniform(arg_keys[10], (NZ, NCOL), jnp.float32) ** block_scale(arg_keys[10], (NZ, NCOL), ((0, 4), (1, 32)), -0.2, 0.2), 0.0, 4.0),
        "flame_flags": plant((jax.random.randint(arg_keys[11], (NTZ, NTC), 0, 2) < 1).astype(jnp.int32), jax.random.fold_in(arg_keys[11], 1), 0, 1),
    }


viscous = 0.05
step_size = 0.25
thicken = 5.0


def face_fill(face_values, tile_edge, direction):
    lead = face_values.shape[0]
    species = face_values.shape[1]
    cells = tile_edge ** 3
    if direction == 0:
        spread = jnp.broadcast_to(face_values[:, :, None, :], (lead, species, tile_edge, tile_edge * tile_edge))
    elif direction == 1:
        shaped = face_values.reshape(lead, species, tile_edge, 1, tile_edge)
        spread = jnp.broadcast_to(shaped, (lead, species, tile_edge, tile_edge, tile_edge))
    else:
        shaped = face_values.reshape(lead, species, tile_edge * tile_edge, 1)
        spread = jnp.broadcast_to(shaped, (lead, species, tile_edge * tile_edge, tile_edge))
    return spread.reshape(lead, species, cells)


def tendency(fields, ghosts, velocity, thickening, rate_matrix, tile_edge):
    face_size = tile_edge * tile_edge
    tile_cells = tile_edge ** 3
    cell_index = jnp.arange(tile_cells, dtype=jnp.int32)
    z_index = cell_index % tile_edge
    y_index = (cell_index // tile_edge) % tile_edge
    x_index = cell_index // face_size
    faces = [face_fill(ghosts[:, :, which * face_size:(which + 1) * face_size], tile_edge, which // 2) for which in range(6)]
    x_low = jnp.where(x_index == 0, faces[0], jnp.roll(fields, face_size, axis=2))
    x_high = jnp.where(x_index == tile_edge - 1, faces[1], jnp.roll(fields, -face_size, axis=2))
    y_low = jnp.where(y_index == 0, faces[2], jnp.roll(fields, tile_edge, axis=2))
    y_high = jnp.where(y_index == tile_edge - 1, faces[3], jnp.roll(fields, -tile_edge, axis=2))
    z_low = jnp.where(z_index == 0, faces[4], jnp.roll(fields, 1, axis=2))
    z_high = jnp.where(z_index == tile_edge - 1, faces[5], jnp.roll(fields, -1, axis=2))
    laplace = x_low + x_high + y_low + y_high + z_low + z_high - 6.0 * fields
    advection = 0.5 * (velocity[0][:, None, None] * (x_high - x_low)
                       + velocity[1][:, None, None] * (y_high - y_low)
                       + velocity[2][:, None, None] * (z_high - z_low))
    burning = fields[:, 0] * fields[:, 1]
    reaction = jnp.einsum("sk,nkc->nsc", rate_matrix, fields * burning[:, None, :], precision=lax.Precision.HIGHEST)
    thick_slot = thickening[:, None, None]
    return thick_slot * viscous * laplace - advection + reaction / thick_slot


def gauss_total(reach):
    sigma = reach / 2.0
    offsets = jnp.arange(-reach, reach + 1).astype(jnp.float32)
    return jnp.sum(jnp.exp(-offsets * offsets / (2.0 * sigma * sigma)))


def circulant(length, reach):
    sigma = reach / 2.0
    row_index = jnp.arange(length, dtype=jnp.int32)[:, None]
    col_index = jnp.arange(length, dtype=jnp.int32)[None, :]
    offset = (col_index - row_index) % length
    distance = jnp.minimum(offset, length - offset).astype(jnp.float32)
    weights = jnp.where(distance <= reach, jnp.exp(-distance * distance / (2.0 * sigma * sigma)), 0.0)
    return (weights / gauss_total(reach)).astype(jnp.float32)


def tile_thickening(filtered, tile_edge, tile_rows, tile_cols):
    clipped = jnp.minimum(filtered, 1.0)
    shaped = clipped.reshape(tile_rows, tile_edge, tile_cols, tile_edge * tile_edge)
    return 1.0 + (thicken - 1.0) * jnp.mean(shaped, axis=(1, 3))


def reference(fields, ghosts, velocity, rate_matrix, recent_tend, older_tend, destination, target_slot, live_counts, tile_ids, sensor, flame_flags):
    peer_count = N_MIG * N_PEN
    expand = jnp.repeat(jnp.repeat(flame_flags.astype(jnp.float32), TE, axis=0), TE * TE, axis=1)
    raw_sensor = sensor * expand
    filtered = jnp.dot(circulant(NZ, BZ), raw_sensor, precision=lax.Precision.HIGHEST)
    thick_grid = tile_thickening(filtered, TE, NTZ, NTC)
    thick_table = thick_grid.reshape(N_PEN, TZ, N_GRP * N_MIG, TCOL).transpose(2, 0, 1, 3).reshape(NTILES)
    slot_thick = jnp.take(thick_table, tile_ids)
    old_index = jnp.arange(NTILES, dtype=jnp.int32)
    group_index = old_index // (SLOTS * peer_count)
    target = (group_index * peer_count + destination) * SLOTS + target_slot
    target = jnp.where(target_slot < SLOTS, target, NTILES).astype(jnp.int32)
    moved_recent = jnp.zeros_like(recent_tend).at[target].set(recent_tend, mode="drop")
    moved_older = jnp.zeros_like(older_tend).at[target].set(older_tend, mode="drop")
    live_mask = ((old_index % SLOTS) < jnp.repeat(live_counts, SLOTS)).astype(jnp.float32)
    device_count = NTILES // SLOTS
    tile_cells = TE ** 3

    def per_device(bundle):
        here_fields, here_ghosts, here_velocity, here_thick, here_recent, here_older, here_live = bundle
        tendencies = tendency(here_fields, here_ghosts, here_velocity, here_thick, rate_matrix, TE)
        update = (23.0 / 12.0) * tendencies - (16.0 / 12.0) * here_recent.astype(jnp.float32) + (5.0 / 12.0) * here_older.astype(jnp.float32)
        mask_column = here_live[:, None, None]
        new_fields = (here_fields + step_size * update) * mask_column
        new_tend = (tendencies * mask_column).astype(jnp.bfloat16)
        return new_fields, new_tend

    bundle = (fields.reshape(device_count, SLOTS, S, tile_cells),
              ghosts.reshape(device_count, SLOTS, S, 6 * TE * TE),
              velocity.reshape(3, device_count, SLOTS).transpose(1, 0, 2),
              slot_thick.reshape(device_count, SLOTS),
              moved_recent.reshape(device_count, SLOTS, S, tile_cells),
              moved_older.reshape(device_count, SLOTS, S, tile_cells),
              live_mask.reshape(device_count, SLOTS))
    new_fields, new_tend = lax.map(per_device, bundle)
    return new_fields.reshape(NTILES, S, tile_cells), new_tend.reshape(NTILES, S, tile_cells), filtered
```

```python
import functools
import math

import jax
import jax.numpy as jnp
from jax import lax
from jax.experimental import pallas as pl
from jax.experimental.pallas import tpu as pltpu
from jax.sharding import PartitionSpec as P

S = 9
SLOTS = 32
CELLS = 4096
HALF = CELLS // 2
FACE = 256
PLANES = 16
BZ = 32
COLS = 4096
ALL_AXES = ("grp", "mig", "pen")
MESH = pl.DeviceIdType.MESH
N_GRP, N_MIG, N_PEN = 8, 4, 4
PEERS = N_MIG * N_PEN

VISCOUS = 0.05
STEP = 0.25
SIGMA = BZ / 2.0
GAUSS_TOTAL = sum(math.exp(-k * k / (2.0 * SIGMA * SIGMA)) for k in range(-BZ, BZ + 1))
CHUNKS = ((0, 3), (3, 6), (6, 9))


def split(x):
    hi = x.astype(jnp.bfloat16)
    return hi, (x - hi.astype(jnp.float32)).astype(jnp.bfloat16)


def iota(shape, dim):
    return lax.broadcasted_iota(jnp.int32, shape, dim)


def column(row):
    same = iota((SLOTS, SLOTS), 0) == iota((SLOTS, SLOTS), 1)
    spread = jnp.broadcast_to(row, (SLOTS, SLOTS))
    return jnp.sum(jnp.where(same, spread, jnp.zeros_like(spread)), axis=1, keepdims=True)


def kernel(
    fields,
    ghosts,
    velocity,
    rate,
    recent,
    older,
    destination,
    target,
    live,
    ids,
    sensor,
    flags,
    new_fields,
    new_tend,
    filtered,
    padded,
    faces,
    rec,
    old,
    out_msg,
    in_msg,
    out_slot,
    in_slot,
    lap,
    adv,
    react,
    sens,
    raw_hi,
    raw_lo,
    prev,
    nxt,
    table,
    vcol,
    local_sem,
    halo_send,
    halo_recv,
    slot_send,
    slot_recv,
    msg_send,
    msg_recv,
    grp_send,
    grp_recv,
    blk_send,
    blk_recv,
):
    g, m, p = (lax.axis_index(a) for a in ALL_AXES)
    group_at = m * N_PEN + p

    def peer(k):
        return (g, lax.rem(m + k // N_PEN, N_MIG), lax.rem(p + k % N_PEN, N_PEN))

    def grp_peer(k):
        return (lax.rem(g + k, N_GRP), m, p)

    in_msg[:, 0:16, :] = jnp.zeros((S, 16, HALF), jnp.bfloat16)
    in_slot[0:8, :] = jnp.full((8, 128), -1.0, jnp.float32)

    barrier = pltpu.get_barrier_semaphore()
    for k in range(1, PEERS):
        pl.semaphore_signal(barrier, inc=1, device_id=peer(k), device_id_type=MESH)
    for k in range(1, N_GRP):
        pl.semaphore_signal(barrier, inc=1, device_id=grp_peer(k), device_id_type=MESH)

    loads = [
        pltpu.make_async_copy(sensor, sens, local_sem.at[0]),
        pltpu.make_async_copy(recent, rec, local_sem.at[1]),
        pltpu.make_async_copy(older, old, local_sem.at[2]),
        pltpu.make_async_copy(fields, padded.at[:, :, FACE : FACE + CELLS], local_sem.at[3]),
        pltpu.make_async_copy(ghosts.at[:, :, 0:FACE], padded.at[:, :, 0:FACE], local_sem.at[4]),
        pltpu.make_async_copy(
            ghosts.at[:, :, FACE : 2 * FACE],
            padded.at[:, :, FACE + CELLS : 2 * FACE + CELLS],
            local_sem.at[5],
        ),
        pltpu.make_async_copy(ghosts.at[:, :, 2 * FACE : 6 * FACE], faces, local_sem.at[6]),
    ]
    for copy in loads:
        copy.start()

    dest = destination[...]
    slot = target[...]
    row_k = iota((2 * PEERS, 4 * SLOTS), 0)
    col_c = iota((2 * PEERS, 4 * SLOTS), 1)
    dest4 = jnp.concatenate([dest] * 4, axis=1)
    k_of = row_k >> 1
    peer_of = ((m + (k_of >> 2)) & 3) * 4 + ((p + (k_of & 3)) & 3)
    hot = (jnp.broadcast_to(dest4, row_k.shape) == peer_of) & (k_of > 0)
    weight = jnp.where((col_c >> 5) & 1 == 0, -16.0, 5.0)
    same_half = (col_c >> 6) == (row_k & 1)
    select = jnp.where(hot & same_half, weight, 0.0).astype(jnp.bfloat16)

    hot32 = hot[:, 0:SLOTS]
    slot_rows = jnp.broadcast_to(slot.astype(jnp.float32), hot32.shape)
    found = jnp.sum(jnp.where(hot32, slot_rows + 1.0, 0.0), axis=1, keepdims=True) - 1.0
    out_slot[...] = jnp.broadcast_to(found, (2 * PEERS, 128))

    live_col = iota((SLOTS, 1), 0) < live[0]
    mask = jnp.where(live_col, 1.0, 0.0)
    keep_row = iota((SLOTS, 2 * SLOTS), 0)
    keep_col = iota((SLOTS, 2 * SLOTS), 1)
    dest2 = jnp.broadcast_to(jnp.concatenate([dest] * 2, axis=1), keep_row.shape)
    slot2 = jnp.broadcast_to(jnp.concatenate([slot] * 2, axis=1), keep_row.shape)
    kept = (dest2 == group_at) & (slot2 == keep_row)
    keep = jnp.where(kept, jnp.where(keep_col < SLOTS, -16.0, 5.0), 0.0).astype(jnp.bfloat16)

    for d in range(3):
        vcol[d] = jnp.broadcast_to(-0.5 * column(velocity[d : d + 1, :]), (SLOTS, 128))

    loads[0].wait()
    for t in range(2):
        for j in range(16):
            flag = flags[t, j].astype(jnp.float32)
            at = (slice(t * 16, t * 16 + 16), slice(j * 256, j * 256 + 256))
            hi, lo = split(sens[at] * flag)
            raw_hi[at] = hi
            raw_lo[at] = lo

    loads[1].wait()
    loads[2].wait()

    @pl.loop(0, S)
    def _(s):
        for c in range(4):
            low = slice(c * 512, c * 512 + 512)
            high = slice(HALF + c * 512, HALF + c * 512 + 512)
            both = jnp.concatenate([rec[s, :, low], old[s, :, low], rec[s, :, high], old[s, :, high]], axis=0)
            out_msg[s, :, low] = jnp.dot(select, both, preferred_element_type=jnp.float32).astype(jnp.bfloat16)

    pl.semaphore_wait(barrier, PEERS - 1 + N_GRP - 1)

    halos = [
        pltpu.make_async_remote_copy(
            raw_hi, prev, halo_send.at[0], halo_recv.at[0], device_id=peer(1), device_id_type=MESH
        ),
        pltpu.make_async_remote_copy(
            raw_hi, nxt, halo_send.at[1], halo_recv.at[1], device_id=peer(3), device_id_type=MESH
        ),
    ]
    for copy in halos:
        copy.start()
    slots = []
    for k in range(1, PEERS):
        rows = slice(2 * k, 2 * k + 2)
        slots.append(
            pltpu.make_async_remote_copy(
                out_slot.at[rows, :], in_slot.at[rows, :], slot_send.at[k], slot_recv.at[k], device_id=peer(k), device_id_type=MESH
            )
        )
    for copy in slots:
        copy.start()
    moves = []
    for c, (s0, s1) in enumerate(CHUNKS):
        for k in range(1, PEERS):
            at = (slice(s0, s1), slice(2 * k, 2 * k + 2), slice(None))
            moves.append(
                pltpu.make_async_remote_copy(
                    out_msg.at[at], in_msg.at[at], msg_send.at[c, k], msg_recv.at[c, k], device_id=peer(k), device_id_type=MESH
                )
            )
    per_chunk = PEERS - 1
    for copy in moves[: 2 * per_chunk]:
        copy.start()

    for copy in loads[3:]:
        copy.wait()
    lane = iota((8, 128), 1)
    lane_z = lane & 15
    first_z = lane_z == 0
    last_z = lane_z == 15
    first_y = lane < 16
    last_y = lane >= 112

    def stencil(step):
        rows = pl.ds(pl.multiple_of((step // PLANES) * 8, 8), 8)
        x = step % PLANES
        at_face = (x // 8) * 128
        in_face = (x % 8) * 16
        idx_y = in_face + lane_z
        idx_z = [in_face + t * 8 + (lane >> 4) for t in range(2)]
        vx, vy, vz = (vcol[d, rows, :] for d in range(3))

        def face(s, which):
            return faces[s, rows, pl.ds(pl.multiple_of(which * FACE + at_face, 128), 128)]

        def plane(s, by, t):
            return padded[s, rows, pl.ds(pl.multiple_of((x + by) * FACE + t * 128, 128), 128)]

        def put(ref, s, t, value):
            ref[s, rows, pl.ds(pl.multiple_of(x * FACE + t * 128, 128), 128)] = value

        def pick(source, idx):
            return jnp.take_along_axis(source, idx, axis=1)

        for s in range(S):
            now = [plane(s, 1, t) for t in range(2)]
            down = [pltpu.roll(v, 16, 1) for v in now]
            up = [pltpu.roll(v, 112, 1) for v in now]
            y_low = [
                jnp.where(first_y, pick(face(s, 0), idx_y), down[0]),
                jnp.where(first_y, down[0], down[1]),
            ]
            y_high = [
                jnp.where(last_y, up[1], up[0]),
                jnp.where(last_y, pick(face(s, 1), idx_y), up[1]),
            ]
            for t in range(2):
                z_low = jnp.where(first_z, pick(face(s, 2), idx_z[t]), pltpu.roll(now[t], 1, 1))
                z_high = jnp.where(last_z, pick(face(s, 3), idx_z[t]), pltpu.roll(now[t], 127, 1))
                x_low = plane(s, 0, t)
                x_high = plane(s, 2, t)
                total = ((x_low + x_high) + (y_low[t] + y_high[t])) + (z_low + z_high)
                put(lap, s, t, VISCOUS * (total - 6.0 * now[t]))
                put(adv, s, t, vx * (x_high - x_low) + vy * (y_high[t] - y_low[t]) + vz * (z_high - z_low))
        for t in range(2):
            f = [plane(s, 1, t) for s in range(S)]
            burning = f[0] * f[1]
            f = [v * burning for v in f]
            for s in range(S):
                total = rate[s, 0] * f[0]
                for k in range(1, S):
                    total = total + rate[s, k] * f[k]
                put(react, s, t, total)

    pl.loop(0, 32)(stencil)

    for copy in halos:
        copy.wait_recv()
    r = iota((BZ, BZ), 0)
    q = iota((BZ, BZ), 1)

    def gauss(offset):
        off = jnp.abs(offset)
        d = off.astype(jnp.float32)
        w = jnp.where(off <= BZ, jnp.exp(-d * d / (2.0 * SIGMA * SIGMA)), 0.0)
        return split(w / GAUSS_TOTAL)

    own_hi, own_lo = gauss(r - q)
    prev_hi, prev_lo = gauss(r + BZ - q)
    next_hi, next_lo = gauss(q + BZ - r)
    bands = jnp.concatenate([own_hi, own_lo, own_hi, prev_hi, prev_lo, next_hi, next_lo], axis=1)
    wide = iota((1, 128), 1)
    sums = jnp.zeros((1, 128), jnp.float32)
    for j in range(16):
        cols = slice(j * 256, j * 256 + 256)
        own, back, ahead = raw_hi[:, cols], prev[:, cols], nxt[:, cols]
        planes = jnp.concatenate([own, own, raw_lo[:, cols], back, back, ahead, ahead], axis=0)
        value = jnp.dot(bands, planes, preferred_element_type=jnp.float32)
        filtered[:, cols] = value
        clipped = jnp.minimum(value, 1.0)
        for t in range(2):
            part = jnp.sum(clipped[t * 16 : t * 16 + 16, :], axis=0, keepdims=True)
            part = jnp.sum(part, axis=1, keepdims=True)
            sums = sums + jnp.where(wide == t * 16 + j, part, 0.0)
    mine = group_at * N_GRP + g
    table[pl.ds(mine, 1), :] = 1.0 + 4.0 * (sums * (1.0 / 4096.0))

    rows_sent = []
    for k in range(1, N_GRP):
        row = table.at[pl.ds(mine, 1), :]
        rows_sent.append(
            pltpu.make_async_remote_copy(row, row, grp_send.at[k], grp_recv.at[k], device_id=grp_peer(k), device_id_type=MESH)
        )
    for copy in rows_sent:
        copy.start()

    pl.loop(32, 48)(stencil)

    for copy in rows_sent:
        copy.wait()
    blocks = []
    block = table.at[pl.ds(pl.multiple_of(group_at * N_GRP, N_GRP), N_GRP), :]
    for k in range(1, PEERS):
        blocks.append(
            pltpu.make_async_remote_copy(block, block, blk_send.at[k], blk_recv.at[k], device_id=peer(k), device_id_type=MESH)
        )
    for copy in blocks:
        copy.start()
    for copy in moves[2 * per_chunk :]:
        copy.start()

    pl.loop(48, 64)(stencil)

    @pl.loop(0, S)
    def _(s):
        for c in range(8):
            cols = slice(c * 512, c * 512 + 512)
            both = jnp.concatenate([rec[s, :, cols], old[s, :, cols]], axis=0)
            stay = jnp.dot(keep, both, preferred_element_type=jnp.float32)
            base = padded[s, :, FACE + c * 512 : FACE + c * 512 + 512]
            new_fields[s, :, cols] = base + (STEP / 12.0) * stay

    for copy in blocks:
        copy.wait()
    id_col = column(ids[...])
    device = id_col >> 5
    row_of = ((device & 15) << 3) + (device >> 4)
    lanes = iota((SLOTS, 128), 1)
    row_hot = jnp.where(lanes == row_of, 1.0, 0.0)
    near = jnp.dot(row_hot, table[...], precision=lax.Precision.HIGHEST, preferred_element_type=jnp.float32)
    thick = jnp.sum(jnp.where(lanes == (id_col & 31), near, 0.0), axis=1, keepdims=True)
    inverse = 1.0 / thick

    for copy in slots:
        copy.wait()
    arrow = iota((2 * PEERS, 128), 0)
    acol = iota((2 * PEERS, 128), 1)
    here = (in_slot[...] == (acol & 31).astype(jnp.float32)) & ((acol >> 5) == (arrow & 1))
    place = jnp.where(here, 1.0, 0.0).T[0 : 2 * SLOTS, :]
    place = (place * jnp.concatenate([mask, mask], axis=0)).astype(jnp.bfloat16)

    for c, (s0, s1) in enumerate(CHUNKS):
        for copy in moves[c * per_chunk : (c + 1) * per_chunk]:
            copy.wait_recv()

        @pl.loop(s0, s1)
        def _(s):
            for n in range(4):
                moved = jnp.dot(place, in_msg[s, :, n * 512 : n * 512 + 512], preferred_element_type=jnp.float32)
                for h in range(2):
                    cols = slice(h * HALF + n * 512, h * HALF + n * 512 + 512)
                    tend = lap[s, :, cols] * thick + adv[s, :, cols] + react[s, :, cols] * inverse
                    new_tend[s, :, cols] = (tend * mask).astype(jnp.bfloat16)
                    part = new_fields[s, :, cols] + (STEP * 23.0 / 12.0) * tend
                    new_fields[s, :, cols] = part * mask + (STEP / 12.0) * moved[h * SLOTS : (h + 1) * SLOTS, :]

    for copy in halos:
        copy.wait_send()
    for copy in moves:
        copy.wait_send()


def local(fields, ghosts, velocity, rate, recent, older, destination, target, live, ids, sensor, flags):
    fields, ghosts, recent, older = (a.transpose(1, 0, 2) for a in (fields, ghosts, recent, older))
    vmem = pl.BlockSpec(memory_space=pltpu.VMEM)
    smem = pl.BlockSpec(memory_space=pltpu.SMEM)
    hbm = pl.BlockSpec(memory_space=pl.ANY)
    dma = pltpu.SemaphoreType.DMA
    f32, bf16 = jnp.float32, jnp.bfloat16
    new_fields, new_tend, filtered = pl.pallas_call(
        kernel,
        out_shape=(
            jax.ShapeDtypeStruct((S, SLOTS, CELLS), f32),
            jax.ShapeDtypeStruct((S, SLOTS, CELLS), bf16),
            jax.ShapeDtypeStruct((BZ, COLS), f32),
        ),
        in_specs=[hbm, hbm, vmem, smem, hbm, hbm, vmem, vmem, smem, vmem, hbm, smem],
        out_specs=(vmem, vmem, vmem),
        scratch_shapes=[
            pltpu.VMEM((S, SLOTS, CELLS + 2 * FACE), f32),
            pltpu.VMEM((S, SLOTS, 4 * FACE), f32),
            pltpu.VMEM((S, SLOTS, CELLS), bf16),
            pltpu.VMEM((S, SLOTS, CELLS), bf16),
            pltpu.VMEM((S, 2 * PEERS, HALF), bf16),
            pltpu.VMEM((S, 2 * PEERS, HALF), bf16),
            pltpu.VMEM((2 * PEERS, 128), f32),
            pltpu.VMEM((2 * PEERS, 128), f32),
            pltpu.VMEM((S, SLOTS, CELLS), f32),
            pltpu.VMEM((S, SLOTS, CELLS), f32),
            pltpu.VMEM((S, SLOTS, CELLS), f32),
            pltpu.VMEM((BZ, COLS), f32),
            pltpu.VMEM((BZ, COLS), bf16),
            pltpu.VMEM((BZ, COLS), bf16),
            pltpu.VMEM((BZ, COLS), bf16),
            pltpu.VMEM((BZ, COLS), bf16),
            pltpu.VMEM((N_GRP * PEERS, 128), f32),
            pltpu.VMEM((3, SLOTS, 128), f32),
            dma((7,)),
            dma((2,)),
            dma((2,)),
            dma((PEERS,)),
            dma((PEERS,)),
            dma((len(CHUNKS), PEERS)),
            dma((len(CHUNKS), PEERS)),
            dma((N_GRP,)),
            dma((N_GRP,)),
            dma((PEERS,)),
            dma((PEERS,)),
        ],
        compiler_params=pltpu.CompilerParams(
            collective_id=0, has_side_effects=True, vmem_limit_bytes=VMEM_LIMIT
        ),
        name="repartition_step",
    )(
        fields,
        ghosts,
        velocity,
        rate,
        recent,
        older,
        destination.reshape(1, SLOTS),
        target.reshape(1, SLOTS),
        live,
        ids.reshape(1, SLOTS),
        sensor,
        flags,
    )
    return new_fields.transpose(1, 0, 2), new_tend.transpose(1, 0, 2), filtered


VMEM_LIMIT = 44 << 20


def solution(mesh):
    tile = P(ALL_AXES, None, None)
    brick = P("pen", ("grp", "mig"))
    flat = P(ALL_AXES)
    return jax.shard_map(
        local,
        mesh=mesh,
        in_specs=(tile, tile, P(None, ALL_AXES), P(), tile, tile, flat, flat, flat, flat, brick, brick),
        out_specs=(tile, tile, brick),
        check_vma=False,
    )
```

```python
import functools
import math

import jax
import jax.numpy as jnp
from jax import lax
from jax.experimental import pallas as pl
from jax.experimental.pallas import tpu as pltpu
from jax.sharding import PartitionSpec as P

S = 9
SLOTS = 32
CELLS = 4096
HALF = CELLS // 2
FACE = 256
PLANES = 16
BZ = 32
COLS = 4096
ALL_AXES = ("grp", "mig", "pen")
MESH = pl.DeviceIdType.MESH
N_GRP, N_MIG, N_PEN = 8, 4, 4
PEERS = N_MIG * N_PEN

VISCOUS = 0.05
STEP = 0.25
SIGMA = BZ / 2.0
GAUSS_TOTAL = sum(math.exp(-k * k / (2.0 * SIGMA * SIGMA)) for k in range(-BZ, BZ + 1))
CHUNKS = ((0, 5), (5, 9))
CUT = (0, 8, 36)
LATER = 24


def split(x):
    hi = x.astype(jnp.bfloat16)
    return hi, (x - hi.astype(jnp.float32)).astype(jnp.bfloat16)


def iota(shape, dim):
    return lax.broadcasted_iota(jnp.int32, shape, dim)


def column(row):
    same = iota((SLOTS, SLOTS), 0) == iota((SLOTS, SLOTS), 1)
    spread = jnp.broadcast_to(row, (SLOTS, SLOTS))
    return jnp.sum(jnp.where(same, spread, jnp.zeros_like(spread)), axis=1, keepdims=True)


def kernel(
    fields,
    ghosts,
    velocity_hbm,
    rate_hbm,
    recent,
    older,
    destination_hbm,
    target_hbm,
    ids_hbm,
    sensor,
    flags_hbm,
    new_fields,
    new_tend,
    filtered,
    padded,
    faces,
    rec,
    old,
    out_msg,
    in_msg,
    out_slot,
    in_slot,
    lap,
    adv,
    react,
    sens,
    raw_hi,
    raw_lo,
    prev,
    nxt,
    table,
    vcol,
    z_face,
    z_terms,
    z_place,
    velocity,
    rate,
    destination,
    target,
    ids,
    flags,
    local_sem,
    small_sem,
    halo_send,
    halo_recv,
    slot_send,
    slot_recv,
    msg_send,
    msg_recv,
    grp_send,
    grp_recv,
    blk_send,
    blk_recv,
    known,
    mix_f,
    mix,
):
    g, m, p = (lax.axis_index(a) for a in ALL_AXES)
    group_at = m * N_PEN + p

    def peer(k):
        return (g, lax.rem(m + k // N_PEN, N_MIG), lax.rem(p + k % N_PEN, N_PEN))

    def grp_peer(k):
        return (lax.rem(g + k, N_GRP), m, p)

    in_msg[:, 0:16, :] = jnp.zeros((S, 16, HALF), jnp.bfloat16)
    in_slot[0:8, :] = jnp.full((8, 128), -1.0, jnp.float32)

    barrier = pltpu.get_barrier_semaphore()
    near = [peer(1), peer(3), peer(4), peer(12), grp_peer(2), grp_peer(6), (g + 1 - 2 * lax.rem(g, 2), m, p)]
    for device in near:
        pl.semaphore_signal(barrier, inc=1, device_id=device, device_id_type=MESH)

    loads = [
        pltpu.make_async_copy(sensor, sens, local_sem.at[0]),
        pltpu.make_async_copy(recent, rec, local_sem.at[1]),
        pltpu.make_async_copy(older, old, local_sem.at[2]),
        pltpu.make_async_copy(fields, padded.at[:, :, FACE : FACE + CELLS], local_sem.at[3]),
        pltpu.make_async_copy(ghosts.at[:, :, 0:FACE], padded.at[:, :, 0:FACE], local_sem.at[4]),
        pltpu.make_async_copy(
            ghosts.at[:, :, FACE : 2 * FACE],
            padded.at[:, :, FACE + CELLS : 2 * FACE + CELLS],
            local_sem.at[5],
        ),
        pltpu.make_async_copy(ghosts.at[:, :, 2 * FACE : 6 * FACE], faces, local_sem.at[6]),
    ]
    small = (
        (flags_hbm, flags),
        (destination_hbm, destination),
        (target_hbm, target),
        (velocity_hbm, velocity),
        (ids_hbm, ids),
        (rate_hbm, rate),
    )
    small = [pltpu.make_async_copy(a, b, small_sem.at[i]) for i, (a, b) in enumerate(small)]
    for copy in loads[:1] + small + loads[1:]:
        copy.start()
    for copy in small:
        copy.wait()

    dest = destination[...]
    slot = target[...]
    row_k = iota((2 * PEERS, 4 * SLOTS), 0)
    col_c = iota((2 * PEERS, 4 * SLOTS), 1)
    dest4 = jnp.concatenate([dest] * 4, axis=1)
    k_of = row_k >> 1
    peer_of = ((m + (k_of >> 2)) & 3) * 4 + ((p + (k_of & 3)) & 3)
    hot = (jnp.broadcast_to(dest4, row_k.shape) == peer_of) & (k_of > 0)
    weight = jnp.where((col_c >> 5) & 1 == 0, -16.0, 5.0)
    same_half = (col_c >> 6) == (row_k & 1)
    select = jnp.where(hot & same_half, weight, 0.0).astype(jnp.bfloat16)

    hot32 = hot[:, 0:SLOTS]
    slot_rows = jnp.broadcast_to(slot.astype(jnp.float32), hot32.shape)
    found = jnp.sum(jnp.where(hot32, slot_rows + 1.0, 0.0), axis=1, keepdims=True) - 1.0
    out_slot[...] = jnp.broadcast_to(found, (2 * PEERS, 128))

    keep_row = iota((SLOTS, 2 * SLOTS), 0)
    keep_col = iota((SLOTS, 2 * SLOTS), 1)
    dest2 = jnp.broadcast_to(jnp.concatenate([dest] * 2, axis=1), keep_row.shape)
    slot2 = jnp.broadcast_to(jnp.concatenate([slot] * 2, axis=1), keep_row.shape)
    kept = (dest2 == group_at) & (slot2 == keep_row)
    stays = jnp.sum(jnp.where(kept[:, 0:SLOTS], 1.0, 0.0), axis=1, keepdims=True)
    keep = jnp.where(kept, jnp.where(keep_col < SLOTS, -16.0, 5.0), 0.0).astype(jnp.bfloat16)

    for d in range(3):
        vcol[d] = jnp.broadcast_to(-0.5 * column(velocity[d : d + 1, :]), (SLOTS, 128))

    z_place[...] = jnp.zeros((8, 512, FACE), jnp.bfloat16)
    zy = iota((16, FACE), 0)
    zc = iota((16, FACE), 1)
    for part in range(4):
        at_end = (zc & 15) == (0 if part < 2 else 15)
        spot = jnp.where((zy == (zc >> 4)) & at_end, 1.0, 0.0).astype(jnp.bfloat16)
        for x in range(8):
            z_place[x, part * 128 + x * 16 : part * 128 + x * 16 + 16, :] = spot

    at = iota((8, FACE), 1)
    part = jnp.where(at < 80, 0, jnp.where(at < 160, 1, 2))
    at = at - 80 * part
    own = ((at & 7) == iota((8, FACE), 0)) & (part * 80 + at < 240)
    for s in range(S):
        row = jnp.zeros((8, FACE), jnp.float32)
        for k in range(S):
            row = jnp.where((at >> 3) == k, rate[s, k], row)
        row = jnp.where(own, row, 0.0)
        high = row.astype(jnp.bfloat16).astype(jnp.float32)
        mix_f[s * 8 : s * 8 + 8, :] = jnp.where(part < 2, high, row - high)
    mix[...] = mix_f[:, 0:240].astype(jnp.bfloat16)

    loads[0].wait()
    for t in range(2):
        for j in range(16):
            flag = flags[t, j].astype(jnp.float32)
            at = (slice(t * 16, t * 16 + 16), slice(j * 256, j * 256 + 256))
            hi, lo = split(sens[at] * flag)
            raw_hi[at] = hi
            raw_lo[at] = lo

    loads[1].wait()
    loads[2].wait()

    @pl.loop(0, S)
    def _(s):
        for c in range(4):
            low = slice(c * 512, c * 512 + 512)
            high = slice(HALF + c * 512, HALF + c * 512 + 512)
            both = jnp.concatenate([rec[s, :, low], old[s, :, low], rec[s, :, high], old[s, :, high]], axis=0)
            out_msg[s, :, low] = jnp.dot(select, both, preferred_element_type=jnp.float32).astype(jnp.bfloat16)

    pl.semaphore_wait(barrier, len(near))

    halos = [
        pltpu.make_async_remote_copy(
            raw_hi, prev, halo_send.at[0], halo_recv.at[0], device_id=peer(1), device_id_type=MESH
        ),
        pltpu.make_async_remote_copy(
            raw_hi, nxt, halo_send.at[1], halo_recv.at[1], device_id=peer(3), device_id_type=MESH
        ),
    ]
    for copy in halos:
        copy.start()
    loads[6].wait()
    for h in range(2):
        for f in range(2):
            at = (2 + f) * FACE + h * 128
            hi, lo = split(faces[:, :, at : at + 128].reshape(S * SLOTS, 128))
            z_terms[h, :, f * 256 : f * 256 + 128] = hi
            z_terms[h, :, f * 256 + 128 : f * 256 + 256] = lo

    def z_plane(x):
        spread = jnp.dot(z_terms[x // 8], z_place[x % 8], preferred_element_type=jnp.float32)
        z_face[:, :, pl.ds(pl.multiple_of(x * FACE, FACE), FACE)] = spread.reshape(S, SLOTS, FACE)

    for r in range(3):
        for device in near:
            pl.semaphore_signal(known.at[r], inc=1, device_id=device, device_id_type=MESH)
        pl.loop((0, 5, 10)[r], (5, 10, 16)[r])(z_plane)
        pl.semaphore_wait(known.at[r], len(near))

    slots = []
    for k in range(1, PEERS):
        rows = slice(2 * k, 2 * k + 2)
        slots.append(
            pltpu.make_async_remote_copy(
                out_slot.at[rows, :], in_slot.at[rows, :], slot_send.at[k], slot_recv.at[k], device_id=peer(k), device_id_type=MESH
            )
        )
    for copy in slots:
        copy.start()
    moves = []
    for c, (s0, s1) in enumerate(CHUNKS):
        for k in range(1, PEERS):
            at = (slice(s0, s1), slice(2 * k, 2 * k + 2), slice(None))
            moves.append(
                pltpu.make_async_remote_copy(
                    out_msg.at[at], in_msg.at[at], msg_send.at[c, k], msg_recv.at[c, k], device_id=peer(k), device_id_type=MESH
                )
            )
    per_chunk = PEERS - 1
    along_x = [copy for i, copy in enumerate(moves) if (i % per_chunk + 1) % N_PEN == 0]
    rest = [copy for i, copy in enumerate(moves) if (i % per_chunk + 1) % N_PEN != 0]
    for copy in along_x:
        copy.start()

    for copy in loads[3:6]:
        copy.wait()
    lane = iota((8, 128), 1)
    lane_z = lane & 15
    first_z = lane_z == 0
    last_z = lane_z == 15
    first_y = lane < 16
    last_y = lane >= 112

    def stencil(step):
        rows = pl.ds(pl.multiple_of((step // PLANES) * 8, 8), 8)
        x = step % PLANES
        at_face = (x // 8) * 128
        in_face = (x % 8) * 16
        to_first = lax.rem(128 - in_face, 128)
        to_last = lax.rem(240 - in_face, 128)
        vx, vy, vz = (vcol[d, rows, :] for d in range(3))

        def face(s, which):
            return faces[s, rows, pl.ds(pl.multiple_of(which * FACE + at_face, 128), 128)]

        def plane(s, by, t):
            return padded[s, rows, pl.ds(pl.multiple_of((x + by) * FACE + t * 128, 128), 128)]

        def put(ref, s, t, value):
            ref[s, rows, pl.ds(pl.multiple_of(x * FACE + t * 128, 128), 128)] = value

        for s in range(S):
            now = [plane(s, 1, t) for t in range(2)]
            down = [pltpu.roll(v, 16, 1) for v in now]
            up = [pltpu.roll(v, 112, 1) for v in now]
            y_low = [
                jnp.where(first_y, pltpu.roll(face(s, 0), to_first, 1), down[0]),
                jnp.where(first_y, down[0], down[1]),
            ]
            y_high = [
                jnp.where(last_y, up[1], up[0]),
                jnp.where(last_y, pltpu.roll(face(s, 1), to_last, 1), up[1]),
            ]
            for t in range(2):
                edge = z_face[s, rows, pl.ds(pl.multiple_of(x * FACE + t * 128, 128), 128)]
                z_low = jnp.where(first_z, edge, pltpu.roll(now[t], 1, 1))
                z_high = jnp.where(last_z, edge, pltpu.roll(now[t], 127, 1))
                x_low = plane(s, 0, t)
                x_high = plane(s, 2, t)
                total = ((x_low + x_high) + (y_low[t] + y_high[t])) + (z_low + z_high)
                put(lap, s, t, total - 6.0 * now[t])
                put(adv, s, t, vx * (x_high - x_low) + vy * (y_high[t] - y_low[t]) + vz * (z_high - z_low))
        here = pl.ds(pl.multiple_of((x + 1) * FACE, FACE), FACE)
        f = [padded[s, rows, here] for s in range(S)]
        burning = f[0] * f[1]
        f = jnp.concatenate([v * burning for v in f] + [jnp.zeros_like(burning)], axis=0)
        hi, lo = split(f)
        mixed = jnp.dot(mix[...], jnp.concatenate([hi, lo, hi], axis=0), preferred_element_type=jnp.float32)
        for s in range(S):
            react[s, rows, pl.ds(pl.multiple_of(x * FACE, FACE), FACE)] = mixed[s * 8 : s * 8 + 8, :]

    pl.loop(0, CUT[0])(stencil)
    for copy in halos:
        copy.wait_send()
    for copy in rest[:LATER]:
        copy.start()
    pl.loop(CUT[0], CUT[1])(stencil)

    for copy in halos:
        copy.wait_recv()
    r = iota((BZ, BZ), 0)
    q = iota((BZ, BZ), 1)

    def gauss(offset):
        off = jnp.abs(offset)
        d = off.astype(jnp.float32)
        w = jnp.where(off <= BZ, jnp.exp(-d * d / (2.0 * SIGMA * SIGMA)), 0.0)
        return split(w / GAUSS_TOTAL)

    own_hi, own_lo = gauss(r - q)
    prev_hi, prev_lo = gauss(r + BZ - q)
    next_hi, next_lo = gauss(q + BZ - r)
    bands = jnp.concatenate([own_hi, own_lo, own_hi, prev_hi, prev_lo, next_hi, next_lo], axis=1)
    wide = iota((1, 128), 1)
    sums = jnp.zeros((1, 128), jnp.float32)
    for j in range(16):
        cols = slice(j * 256, j * 256 + 256)
        own, back, ahead = raw_hi[:, cols], prev[:, cols], nxt[:, cols]
        planes = jnp.concatenate([own, own, raw_lo[:, cols], back, back, ahead, ahead], axis=0)
        value = jnp.dot(bands, planes, preferred_element_type=jnp.float32)
        filtered[:, cols] = value
        clipped = jnp.minimum(value, 1.0)
        for t in range(2):
            part = jnp.sum(clipped[t * 16 : t * 16 + 16, :], axis=0, keepdims=True)
            part = jnp.sum(part, axis=1, keepdims=True)
            sums = sums + jnp.where(wide == t * 16 + j, part, 0.0)
    mine = group_at * N_GRP + g
    table[pl.ds(mine, 1), :] = 1.0 + 4.0 * (sums * (1.0 / 4096.0))

    rows_sent = []
    for k in range(1, N_GRP):
        row = table.at[pl.ds(mine, 1), :]
        rows_sent.append(
            pltpu.make_async_remote_copy(row, row, grp_send.at[k], grp_recv.at[k], device_id=grp_peer(k), device_id_type=MESH)
        )
    for copy in rows_sent:
        copy.start()

    pl.loop(CUT[1], CUT[2])(stencil)

    for copy in rows_sent:
        copy.wait()
    blocks = []
    block = table.at[pl.ds(pl.multiple_of(group_at * N_GRP, N_GRP), N_GRP), :]
    for k in range(1, PEERS):
        blocks.append(
            pltpu.make_async_remote_copy(block, block, blk_send.at[k], blk_recv.at[k], device_id=peer(k), device_id_type=MESH)
        )
    for copy in blocks:
        copy.start()
    for copy in rest[LATER:]:
        copy.start()

    pl.loop(CUT[2], 64)(stencil)

    @pl.loop(0, S)
    def _(s):
        for c in range(8):
            cols = slice(c * 512, c * 512 + 512)
            both = jnp.concatenate([rec[s, :, cols], old[s, :, cols]], axis=0)
            stay = jnp.dot(keep, both, preferred_element_type=jnp.float32)
            base = padded[s, :, FACE + c * 512 : FACE + c * 512 + 512]
            new_fields[s, :, cols] = base + (STEP / 12.0) * stay

    for copy in blocks:
        copy.wait()
    id_col = column(ids[...])
    device = id_col >> 5
    row_of = ((device & 15) << 3) + (device >> 4)
    lanes = iota((SLOTS, 128), 1)
    row_hot = jnp.where(lanes == row_of, 1.0, 0.0)
    near = jnp.dot(row_hot, table[...], precision=lax.Precision.HIGHEST, preferred_element_type=jnp.float32)
    thick = jnp.sum(jnp.where(lanes == (id_col & 31), near, 0.0), axis=1, keepdims=True)
    inverse = 1.0 / thick
    spreading = VISCOUS * thick

    for copy in slots:
        copy.wait()
    arrow = iota((2 * PEERS, 128), 0)
    acol = iota((2 * PEERS, 128), 1)
    here = (in_slot[...] == (acol & 31).astype(jnp.float32)) & ((acol >> 5) == (arrow & 1))
    place = jnp.where(here, 1.0, 0.0).T[0 : 2 * SLOTS, :]
    mask = stays + jnp.sum(place[0:SLOTS, :], axis=1, keepdims=True)
    place = place.astype(jnp.bfloat16)

    for c, (s0, s1) in enumerate(CHUNKS):
        for copy in moves[c * per_chunk : (c + 1) * per_chunk]:
            copy.wait_recv()

        @pl.loop(s0, s1)
        def _(s):
            for n in range(4):
                moved = jnp.dot(place, in_msg[s, :, n * 512 : n * 512 + 512], preferred_element_type=jnp.float32)
                for h in range(2):
                    cols = slice(h * HALF + n * 512, h * HALF + n * 512 + 512)
                    tend = lap[s, :, cols] * spreading + adv[s, :, cols] + react[s, :, cols] * inverse
                    new_tend[s, :, cols] = (tend * mask).astype(jnp.bfloat16)
                    part = new_fields[s, :, cols] + (STEP * 23.0 / 12.0) * tend
                    new_fields[s, :, cols] = part * mask + (STEP / 12.0) * moved[h * SLOTS : (h + 1) * SLOTS, :]

    for copy in moves:
        copy.wait_send()


def local(fields, ghosts, velocity, rate, recent, older, destination, target, live, ids, sensor, flags):
    fields, ghosts, recent, older = (a.transpose(1, 0, 2) for a in (fields, ghosts, recent, older))
    rows = (a.reshape(1, SLOTS) for a in (destination, target, ids))
    destination, target, ids = rows
    args = (fields, ghosts, velocity, rate, recent, older, destination, target, ids, sensor, flags)
    vmem = pl.BlockSpec(memory_space=pltpu.VMEM)
    hbm = pl.BlockSpec(memory_space=pltpu.HBM)
    dma = pltpu.SemaphoreType.DMA
    f32, bf16 = jnp.float32, jnp.bfloat16
    new_fields, new_tend, filtered = pl.pallas_call(
        kernel,
        out_shape=(
            jax.ShapeDtypeStruct((S, SLOTS, CELLS), f32),
            jax.ShapeDtypeStruct((S, SLOTS, CELLS), bf16),
            jax.ShapeDtypeStruct((BZ, COLS), f32),
        ),
        in_specs=[hbm] * 11,
        out_specs=(vmem, vmem, vmem),
        scratch_shapes=[
            pltpu.VMEM((S, SLOTS, CELLS + 2 * FACE), f32),
            pltpu.VMEM((S, SLOTS, 4 * FACE), f32),
            pltpu.VMEM((S, SLOTS, CELLS), bf16),
            pltpu.VMEM((S, SLOTS, CELLS), bf16),
            pltpu.VMEM((S, 2 * PEERS, HALF), bf16),
            pltpu.VMEM((S, 2 * PEERS, HALF), bf16),
            pltpu.VMEM((2 * PEERS, 128), f32),
            pltpu.VMEM((2 * PEERS, 128), f32),
            pltpu.VMEM((S, SLOTS, CELLS), f32),
            pltpu.VMEM((S, SLOTS, CELLS), f32),
            pltpu.VMEM((S, SLOTS, CELLS), f32),
            pltpu.VMEM((BZ, COLS), f32),
            pltpu.VMEM((BZ, COLS), bf16),
            pltpu.VMEM((BZ, COLS), bf16),
            pltpu.VMEM((BZ, COLS), bf16),
            pltpu.VMEM((BZ, COLS), bf16),
            pltpu.VMEM((N_GRP * PEERS, 128), f32),
            pltpu.VMEM((3, SLOTS, 128), f32),
            pltpu.VMEM((S, SLOTS, CELLS), f32),
            pltpu.VMEM((2, S * SLOTS, 512), bf16),
            pltpu.VMEM((8, 512, FACE), bf16),
            pltpu.VMEM((3, SLOTS), f32),
            pltpu.SMEM((S, S), f32),
            pltpu.VMEM((1, SLOTS), jnp.int32),
            pltpu.VMEM((1, SLOTS), jnp.int32),
            pltpu.VMEM((1, SLOTS), jnp.int32),
            pltpu.SMEM((2, 16), jnp.int32),
            dma((7,)),
            dma((7,)),
            dma((2,)),
            dma((2,)),
            dma((PEERS,)),
            dma((PEERS,)),
            dma((len(CHUNKS), PEERS)),
            dma((len(CHUNKS), PEERS)),
            dma((N_GRP,)),
            dma((N_GRP,)),
            dma((PEERS,)),
            dma((PEERS,)),
            pltpu.SemaphoreType.REGULAR((3,)),
            pltpu.VMEM((S * 8, FACE), f32),
            pltpu.VMEM((S * 8, 240), bf16),
        ],
        compiler_params=pltpu.CompilerParams(
            collective_id=0, has_side_effects=True, vmem_limit_bytes=VMEM_LIMIT
        ),
        name="repartition_step",
    )(*(pltpu.with_memory_space_constraint(a, pltpu.HBM) for a in args))
    return new_fields.transpose(1, 0, 2), new_tend.transpose(1, 0, 2), filtered


VMEM_LIMIT = 40 << 20


def solution(mesh):
    tile = P(ALL_AXES, None, None)
    brick = P("pen", ("grp", "mig"))
    flat = P(ALL_AXES)
    return jax.shard_map(
        local,
        mesh=mesh,
        in_specs=(tile, tile, P(None, ALL_AXES), P(), tile, tile, flat, flat, flat, flat, brick, brick),
        out_specs=(tile, tile, brick),
        check_vma=False,
    )
```

```python
import functools
import math

import jax
import jax.numpy as jnp
from jax import lax
from jax.experimental import pallas as pl
from jax.experimental.pallas import tpu as pltpu
from jax.sharding import PartitionSpec as P

S = 9
SLOTS = 32
CELLS = 4096
HALF = CELLS // 2
FACE = 256
PLANES = 16
BZ = 32
COLS = 4096
ALL_AXES = ("grp", "mig", "pen")
MESH = pl.DeviceIdType.MESH
N_GRP, N_MIG, N_PEN = 8, 4, 4
PEERS = N_MIG * N_PEN

VISCOUS = 0.05
STEP = 0.25
SIGMA = BZ / 2.0
GAUSS_TOTAL = sum(math.exp(-k * k / (2.0 * SIGMA * SIGMA)) for k in range(-BZ, BZ + 1))
CHUNKS = ((0, 5), (5, 9))
CUT = (0, 8, 36)
LATER = 24


def split(x):
    hi = x.astype(jnp.bfloat16)
    return hi, (x - hi.astype(jnp.float32)).astype(jnp.bfloat16)


def iota(shape, dim):
    return lax.broadcasted_iota(jnp.int32, shape, dim)


def column(row):
    same = iota((SLOTS, SLOTS), 0) == iota((SLOTS, SLOTS), 1)
    spread = jnp.broadcast_to(row, (SLOTS, SLOTS))
    return jnp.sum(jnp.where(same, spread, jnp.zeros_like(spread)), axis=1, keepdims=True)


def kernel(
    fields,
    ghosts,
    velocity_hbm,
    rate_hbm,
    recent,
    older,
    destination_hbm,
    target_hbm,
    ids_hbm,
    sensor,
    flags_hbm,
    new_fields,
    new_tend,
    filtered,
    padded,
    faces,
    rec,
    old,
    out_msg,
    in_msg,
    out_slot,
    in_slot,
    lap,
    adv,
    react,
    sens,
    raw_hi,
    raw_lo,
    prev,
    nxt,
    table,
    vcol,
    z_face,
    z_terms,
    z_place,
    velocity,
    rate,
    destination,
    target,
    ids,
    flags,
    local_sem,
    small_sem,
    halo_send,
    halo_recv,
    slot_send,
    slot_recv,
    msg_send,
    msg_recv,
    grp_send,
    grp_recv,
    blk_send,
    blk_recv,
    known,
    mix_f,
    mix,
):
    g, m, p = (lax.axis_index(a) for a in ALL_AXES)
    group_at = m * N_PEN + p

    def peer(k):
        return (g, lax.rem(m + k // N_PEN, N_MIG), lax.rem(p + k % N_PEN, N_PEN))

    def grp_peer(k):
        return (lax.rem(g + k, N_GRP), m, p)

    in_msg[:, 0:16, :] = jnp.zeros((S, 16, HALF), jnp.bfloat16)
    in_slot[0:8, :] = jnp.full((8, 128), -1.0, jnp.float32)

    barrier = pltpu.get_barrier_semaphore()
    near = [peer(1), peer(3), peer(4), peer(12), grp_peer(2), grp_peer(6), (g + 1 - 2 * lax.rem(g, 2), m, p)]
    for device in near:
        pl.semaphore_signal(barrier, inc=1, device_id=device, device_id_type=MESH)

    loads = [
        pltpu.make_async_copy(sensor, sens, local_sem.at[0]),
        pltpu.make_async_copy(recent, rec, local_sem.at[1]),
        pltpu.make_async_copy(older, old, local_sem.at[2]),
        pltpu.make_async_copy(fields, padded.at[:, :, FACE : FACE + CELLS], local_sem.at[3]),
        pltpu.make_async_copy(ghosts.at[:, :, 0:FACE], padded.at[:, :, 0:FACE], local_sem.at[4]),
        pltpu.make_async_copy(
            ghosts.at[:, :, FACE : 2 * FACE],
            padded.at[:, :, FACE + CELLS : 2 * FACE + CELLS],
            local_sem.at[5],
        ),
        pltpu.make_async_copy(ghosts.at[:, :, 2 * FACE : 6 * FACE], faces, local_sem.at[6]),
    ]
    small = (
        (flags_hbm, flags),
        (destination_hbm, destination),
        (target_hbm, target),
        (velocity_hbm, velocity),
        (ids_hbm, ids),
        (rate_hbm, rate),
    )
    small = [pltpu.make_async_copy(a, b, small_sem.at[i]) for i, (a, b) in enumerate(small)]
    for copy in loads[:1] + small + loads[1:]:
        copy.start()
    for copy in small:
        copy.wait()

    dest = destination[...]
    slot = target[...]
    row_k = iota((2 * PEERS, 4 * SLOTS), 0)
    col_c = iota((2 * PEERS, 4 * SLOTS), 1)
    dest4 = jnp.concatenate([dest] * 4, axis=1)
    k_of = row_k >> 1
    peer_of = ((m + (k_of >> 2)) & 3) * 4 + ((p + (k_of & 3)) & 3)
    hot = (jnp.broadcast_to(dest4, row_k.shape) == peer_of) & (k_of > 0)
    weight = jnp.where((col_c >> 5) & 1 == 0, -16.0, 5.0)
    same_half = (col_c >> 6) == (row_k & 1)
    select = jnp.where(hot & same_half, weight, 0.0).astype(jnp.bfloat16)

    hot32 = hot[:, 0:SLOTS]
    slot_rows = jnp.broadcast_to(slot.astype(jnp.float32), hot32.shape)
    found = jnp.sum(jnp.where(hot32, slot_rows + 1.0, 0.0), axis=1, keepdims=True) - 1.0
    out_slot[...] = jnp.broadcast_to(found, (2 * PEERS, 128))

    keep_row = iota((SLOTS, 2 * SLOTS), 0)
    keep_col = iota((SLOTS, 2 * SLOTS), 1)
    dest2 = jnp.broadcast_to(jnp.concatenate([dest] * 2, axis=1), keep_row.shape)
    slot2 = jnp.broadcast_to(jnp.concatenate([slot] * 2, axis=1), keep_row.shape)
    kept = (dest2 == group_at) & (slot2 == keep_row)
    stays = jnp.sum(jnp.where(kept[:, 0:SLOTS], 1.0, 0.0), axis=1, keepdims=True)
    keep = jnp.where(kept, jnp.where(keep_col < SLOTS, -16.0, 5.0), 0.0).astype(jnp.bfloat16)

    for d in range(3):
        vcol[d] = jnp.broadcast_to(-0.5 * column(velocity[d : d + 1, :]), (SLOTS, 128))

    z_place[...] = jnp.zeros((8, 512, FACE), jnp.bfloat16)
    zy = iota((16, FACE), 0)
    zc = iota((16, FACE), 1)
    for part in range(4):
        at_end = (zc & 15) == (0 if part < 2 else 15)
        spot = jnp.where((zy == (zc >> 4)) & at_end, 1.0, 0.0).astype(jnp.bfloat16)
        for x in range(8):
            z_place[x, part * 128 + x * 16 : part * 128 + x * 16 + 16, :] = spot

    at = iota((8, FACE), 1)
    part = jnp.where(at < 80, 0, jnp.where(at < 160, 1, 2))
    at = at - 80 * part
    own = ((at & 7) == iota((8, FACE), 0)) & (part * 80 + at < 240)
    for s in range(S):
        row = jnp.zeros((8, FACE), jnp.float32)
        for k in range(S):
            row = jnp.where((at >> 3) == k, rate[s, k], row)
        row = jnp.where(own, row, 0.0)
        high = row.astype(jnp.bfloat16).astype(jnp.float32)
        mix_f[s * 8 : s * 8 + 8, :] = jnp.where(part < 2, high, row - high)
    mix[...] = mix_f[:, 0:240].astype(jnp.bfloat16)

    loads[0].wait()
    for t in range(2):
        for j in range(16):
            flag = flags[t, j].astype(jnp.float32)
            at = (slice(t * 16, t * 16 + 16), slice(j * 256, j * 256 + 256))
            hi, lo = split(sens[at] * flag)
            raw_hi[at] = hi
            raw_lo[at] = lo

    loads[1].wait()
    loads[2].wait()

    def messages(s):
        for c in range(4):
            low = slice(c * 512, c * 512 + 512)
            high = slice(HALF + c * 512, HALF + c * 512 + 512)
            both = jnp.concatenate([rec[s, :, low], old[s, :, low], rec[s, :, high], old[s, :, high]], axis=0)
            out_msg[s, :, low] = jnp.dot(select, both, preferred_element_type=jnp.float32).astype(jnp.bfloat16)

    pl.loop(0, 3)(messages)
    pl.semaphore_wait(barrier, len(near))

    halos = [
        pltpu.make_async_remote_copy(
            raw_hi, prev, halo_send.at[0], halo_recv.at[0], device_id=peer(1), device_id_type=MESH
        ),
        pltpu.make_async_remote_copy(
            raw_hi, nxt, halo_send.at[1], halo_recv.at[1], device_id=peer(3), device_id_type=MESH
        ),
    ]
    for copy in halos:
        copy.start()
    loads[6].wait()
    for h in range(2):
        for f in range(2):
            at = (2 + f) * FACE + h * 128
            hi, lo = split(faces[:, :, at : at + 128].reshape(S * SLOTS, 128))
            z_terms[h, :, f * 256 : f * 256 + 128] = hi
            z_terms[h, :, f * 256 + 128 : f * 256 + 256] = lo

    def z_plane(x):
        spread = jnp.dot(z_terms[x // 8], z_place[x % 8], preferred_element_type=jnp.float32)
        z_face[:, :, pl.ds(pl.multiple_of(x * FACE, FACE), FACE)] = spread.reshape(S, SLOTS, FACE)

    for r in range(3):
        for device in near:
            pl.semaphore_signal(known.at[r], inc=1, device_id=device, device_id_type=MESH)
        pl.loop((3, 5, 7)[r], (5, 7, 9)[r])(messages)
        pl.loop((0, 5, 10)[r], (5, 10, 16)[r])(z_plane)
        pl.semaphore_wait(known.at[r], len(near))

    slots = []
    for k in range(1, PEERS):
        rows = slice(2 * k, 2 * k + 2)
        slots.append(
            pltpu.make_async_remote_copy(
                out_slot.at[rows, :], in_slot.at[rows, :], slot_send.at[k], slot_recv.at[k], device_id=peer(k), device_id_type=MESH
            )
        )
    for copy in slots:
        copy.start()
    moves = []
    for c, (s0, s1) in enumerate(CHUNKS):
        for k in range(1, PEERS):
            at = (slice(s0, s1), slice(2 * k, 2 * k + 2), slice(None))
            moves.append(
                pltpu.make_async_remote_copy(
                    out_msg.at[at], in_msg.at[at], msg_send.at[c, k], msg_recv.at[c, k], device_id=peer(k), device_id_type=MESH
                )
            )
    per_chunk = PEERS - 1
    along_x = [copy for i, copy in enumerate(moves) if (i % per_chunk + 1) % N_PEN == 0]
    rest = [copy for i, copy in enumerate(moves) if (i % per_chunk + 1) % N_PEN != 0]
    for copy in along_x:
        copy.start()

    for copy in loads[3:6]:
        copy.wait()
    lane = iota((8, 128), 1)
    lane_z = lane & 15
    first_z = lane_z == 0
    last_z = lane_z == 15
    first_y = lane < 16
    last_y = lane >= 112

    def stencil(step):
        rows = pl.ds(pl.multiple_of((step // PLANES) * 8, 8), 8)
        x = step % PLANES
        at_face = (x // 8) * 128
        in_face = (x % 8) * 16
        to_first = lax.rem(128 - in_face, 128)
        to_last = lax.rem(240 - in_face, 128)
        vx, vy, vz = (vcol[d, rows, :] for d in range(3))

        def face(s, which):
            return faces[s, rows, pl.ds(pl.multiple_of(which * FACE + at_face, 128), 128)]

        def plane(s, by, t):
            return padded[s, rows, pl.ds(pl.multiple_of((x + by) * FACE + t * 128, 128), 128)]

        def put(ref, s, t, value):
            ref[s, rows, pl.ds(pl.multiple_of(x * FACE + t * 128, 128), 128)] = value

        for s in range(S):
            now = [plane(s, 1, t) for t in range(2)]
            down = [pltpu.roll(v, 16, 1) for v in now]
            up = [pltpu.roll(v, 112, 1) for v in now]
            y_low = [
                jnp.where(first_y, pltpu.roll(face(s, 0), to_first, 1), down[0]),
                jnp.where(first_y, down[0], down[1]),
            ]
            y_high = [
                jnp.where(last_y, up[1], up[0]),
                jnp.where(last_y, pltpu.roll(face(s, 1), to_last, 1), up[1]),
            ]
            for t in range(2):
                edge = z_face[s, rows, pl.ds(pl.multiple_of(x * FACE + t * 128, 128), 128)]
                z_low = jnp.where(first_z, edge, pltpu.roll(now[t], 1, 1))
                z_high = jnp.where(last_z, edge, pltpu.roll(now[t], 127, 1))
                x_low = plane(s, 0, t)
                x_high = plane(s, 2, t)
                total = ((x_low + x_high) + (y_low[t] + y_high[t])) + (z_low + z_high)
                put(lap, s, t, total - 6.0 * now[t])
                put(adv, s, t, vx * (x_high - x_low) + vy * (y_high[t] - y_low[t]) + vz * (z_high - z_low))
        here = pl.ds(pl.multiple_of((x + 1) * FACE, FACE), FACE)
        f = [padded[s, rows, here] for s in range(S)]
        burning = f[0] * f[1]
        f = jnp.concatenate([v * burning for v in f] + [jnp.zeros_like(burning)], axis=0)
        hi, lo = split(f)
        mixed = jnp.dot(mix[...], jnp.concatenate([hi, lo, hi], axis=0), preferred_element_type=jnp.float32)
        for s in range(S):
            react[s, rows, pl.ds(pl.multiple_of(x * FACE, FACE), FACE)] = mixed[s * 8 : s * 8 + 8, :]

    pl.loop(0, CUT[0])(stencil)
    for copy in halos:
        copy.wait_send()
    for copy in rest[:LATER]:
        copy.start()
    pl.loop(CUT[0], CUT[1])(stencil)

    for copy in halos:
        copy.wait_recv()
    r = iota((BZ, BZ), 0)
    q = iota((BZ, BZ), 1)

    def gauss(offset):
        off = jnp.abs(offset)
        d = off.astype(jnp.float32)
        w = jnp.where(off <= BZ, jnp.exp(-d * d / (2.0 * SIGMA * SIGMA)), 0.0)
        return split(w / GAUSS_TOTAL)

    own_hi, own_lo = gauss(r - q)
    prev_hi, prev_lo = gauss(r + BZ - q)
    next_hi, next_lo = gauss(q + BZ - r)
    bands = jnp.concatenate([own_hi, own_lo, own_hi, prev_hi, prev_lo, next_hi, next_lo], axis=1)
    wide = iota((1, 128), 1)
    sums = jnp.zeros((1, 128), jnp.float32)
    for j in range(16):
        cols = slice(j * 256, j * 256 + 256)
        own, back, ahead = raw_hi[:, cols], prev[:, cols], nxt[:, cols]
        planes = jnp.concatenate([own, own, raw_lo[:, cols], back, back, ahead, ahead], axis=0)
        value = jnp.dot(bands, planes, preferred_element_type=jnp.float32)
        filtered[:, cols] = value
        clipped = jnp.minimum(value, 1.0)
        for t in range(2):
            part = jnp.sum(clipped[t * 16 : t * 16 + 16, :], axis=0, keepdims=True)
            part = jnp.sum(part, axis=1, keepdims=True)
            sums = sums + jnp.where(wide == t * 16 + j, part, 0.0)
    mine = group_at * N_GRP + g
    table[pl.ds(mine, 1), :] = 1.0 + 4.0 * (sums * (1.0 / 4096.0))

    rows_sent = []
    for k in range(1, N_GRP):
        row = table.at[pl.ds(mine, 1), :]
        rows_sent.append(
            pltpu.make_async_remote_copy(row, row, grp_send.at[k], grp_recv.at[k], device_id=grp_peer(k), device_id_type=MESH)
        )
    for copy in rows_sent:
        copy.start()

    pl.loop(CUT[1], CUT[2])(stencil)

    for copy in rows_sent:
        copy.wait()
    blocks = []
    block = table.at[pl.ds(pl.multiple_of(group_at * N_GRP, N_GRP), N_GRP), :]
    for k in range(1, PEERS):
        blocks.append(
            pltpu.make_async_remote_copy(block, block, blk_send.at[k], blk_recv.at[k], device_id=peer(k), device_id_type=MESH)
        )
    for copy in blocks:
        copy.start()
    for copy in rest[LATER:]:
        copy.start()

    pl.loop(CUT[2], 64)(stencil)

    @pl.loop(0, S)
    def _(s):
        for c in range(8):
            cols = slice(c * 512, c * 512 + 512)
            both = jnp.concatenate([rec[s, :, cols], old[s, :, cols]], axis=0)
            stay = jnp.dot(keep, both, preferred_element_type=jnp.float32)
            base = padded[s, :, FACE + c * 512 : FACE + c * 512 + 512]
            new_fields[s, :, cols] = base + (STEP / 12.0) * stay

    for copy in blocks:
        copy.wait()
    id_col = column(ids[...])
    device = id_col >> 5
    row_of = ((device & 15) << 3) + (device >> 4)
    lanes = iota((SLOTS, 128), 1)
    row_hot = jnp.where(lanes == row_of, 1.0, 0.0)
    near = jnp.dot(row_hot, table[...], precision=lax.Precision.HIGHEST, preferred_element_type=jnp.float32)
    thick = jnp.sum(jnp.where(lanes == (id_col & 31), near, 0.0), axis=1, keepdims=True)
    inverse = 1.0 / thick
    spreading = VISCOUS * thick

    for copy in slots:
        copy.wait()
    arrow = iota((2 * PEERS, 128), 0)
    acol = iota((2 * PEERS, 128), 1)
    here = (in_slot[...] == (acol & 31).astype(jnp.float32)) & ((acol >> 5) == (arrow & 1))
    place = jnp.where(here, 1.0, 0.0).T[0 : 2 * SLOTS, :]
    mask = stays + jnp.sum(place[0:SLOTS, :], axis=1, keepdims=True)
    place = place.astype(jnp.bfloat16)

    for c, (s0, s1) in enumerate(CHUNKS):
        for copy in moves[c * per_chunk : (c + 1) * per_chunk]:
            copy.wait_recv()

        @pl.loop(s0, s1)
        def _(s):
            for n in range(4):
                moved = jnp.dot(place, in_msg[s, :, n * 512 : n * 512 + 512], preferred_element_type=jnp.float32)
                for h in range(2):
                    cols = slice(h * HALF + n * 512, h * HALF + n * 512 + 512)
                    tend = lap[s, :, cols] * spreading + adv[s, :, cols] + react[s, :, cols] * inverse
                    new_tend[s, :, cols] = (tend * mask).astype(jnp.bfloat16)
                    part = new_fields[s, :, cols] + (STEP * 23.0 / 12.0) * tend
                    new_fields[s, :, cols] = part * mask + (STEP / 12.0) * moved[h * SLOTS : (h + 1) * SLOTS, :]

    for copy in moves:
        copy.wait_send()


def local(fields, ghosts, velocity, rate, recent, older, destination, target, live, ids, sensor, flags):
    fields, ghosts, recent, older = (a.transpose(1, 0, 2) for a in (fields, ghosts, recent, older))
    rows = (a.reshape(1, SLOTS) for a in (destination, target, ids))
    destination, target, ids = rows
    args = (fields, ghosts, velocity, rate, recent, older, destination, target, ids, sensor, flags)
    vmem = pl.BlockSpec(memory_space=pltpu.VMEM)
    hbm = pl.BlockSpec(memory_space=pltpu.HBM)
    dma = pltpu.SemaphoreType.DMA
    f32, bf16 = jnp.float32, jnp.bfloat16
    new_fields, new_tend, filtered = pl.pallas_call(
        kernel,
        out_shape=(
            jax.ShapeDtypeStruct((S, SLOTS, CELLS), f32),
            jax.ShapeDtypeStruct((S, SLOTS, CELLS), bf16),
            jax.ShapeDtypeStruct((BZ, COLS), f32),
        ),
        in_specs=[hbm] * 11,
        out_specs=(vmem, vmem, vmem),
        scratch_shapes=[
            pltpu.VMEM((S, SLOTS, CELLS + 2 * FACE), f32),
            pltpu.VMEM((S, SLOTS, 4 * FACE), f32),
            pltpu.VMEM((S, SLOTS, CELLS), bf16),
            pltpu.VMEM((S, SLOTS, CELLS), bf16),
            pltpu.VMEM((S, 2 * PEERS, HALF), bf16),
            pltpu.VMEM((S, 2 * PEERS, HALF), bf16),
            pltpu.VMEM((2 * PEERS, 128), f32),
            pltpu.VMEM((2 * PEERS, 128), f32),
            pltpu.VMEM((S, SLOTS, CELLS), f32),
            pltpu.VMEM((S, SLOTS, CELLS), f32),
            pltpu.VMEM((S, SLOTS, CELLS), f32),
            pltpu.VMEM((BZ, COLS), f32),
            pltpu.VMEM((BZ, COLS), bf16),
            pltpu.VMEM((BZ, COLS), bf16),
            pltpu.VMEM((BZ, COLS), bf16),
            pltpu.VMEM((BZ, COLS), bf16),
            pltpu.VMEM((N_GRP * PEERS, 128), f32),
            pltpu.VMEM((3, SLOTS, 128), f32),
            pltpu.VMEM((S, SLOTS, CELLS), f32),
            pltpu.VMEM((2, S * SLOTS, 512), bf16),
            pltpu.VMEM((8, 512, FACE), bf16),
            pltpu.VMEM((3, SLOTS), f32),
            pltpu.SMEM((S, S), f32),
            pltpu.VMEM((1, SLOTS), jnp.int32),
            pltpu.VMEM((1, SLOTS), jnp.int32),
            pltpu.VMEM((1, SLOTS), jnp.int32),
            pltpu.SMEM((2, 16), jnp.int32),
            dma((7,)),
            dma((7,)),
            dma((2,)),
            dma((2,)),
            dma((PEERS,)),
            dma((PEERS,)),
            dma((len(CHUNKS), PEERS)),
            dma((len(CHUNKS), PEERS)),
            dma((N_GRP,)),
            dma((N_GRP,)),
            dma((PEERS,)),
            dma((PEERS,)),
            pltpu.SemaphoreType.REGULAR((3,)),
            pltpu.VMEM((S * 8, FACE), f32),
            pltpu.VMEM((S * 8, 240), bf16),
        ],
        compiler_params=pltpu.CompilerParams(
            collective_id=0, has_side_effects=True, vmem_limit_bytes=VMEM_LIMIT
        ),
        name="repartition_step",
    )(*(pltpu.with_memory_space_constraint(a, pltpu.HBM) for a in args))
    return new_fields.transpose(1, 0, 2), new_tend.transpose(1, 0, 2), filtered


VMEM_LIMIT = 40 << 20


def solution(mesh):
    tile = P(ALL_AXES, None, None)
    brick = P("pen", ("grp", "mig"))
    flat = P(ALL_AXES)
    return jax.shard_map(
        local,
        mesh=mesh,
        in_specs=(tile, tile, P(None, ALL_AXES), P(), tile, tile, flat, flat, flat, flat, brick, brick),
        out_specs=(tile, tile, brick),
        check_vma=False,
    )
```
